32 devices in a mesh: rep: 8 (over z, y), tp: 4 (over x, core).
Axes of the slice: x: 2, y: 2, z: 4, core: 2. Of those that a mesh axis runs over, the one named last changes fastest.
Arguments:
- image_grads: bfloat16 [32, 48, 1280], P('rep', 'tp'), may hold values from -6 to 6
- dest_rank: int32 [32], P('rep'), may hold values from 0 to 7, as said below
- dest_slot: int32 [32], P('rep'), may hold values from 0 to 7, as said below
- saved_inputs: bfloat16 [64, 48, 1280], P('rep'), may hold values from -6 to 6
- up_weight: bfloat16 [1280, 5120], P(None, 'tp'), may hold values from -0.15625 to 0.15625
- down_weight: bfloat16 [5120, 1280], P('tp'), may hold values from -0.078125 to 0.078125
- norm_gain: float32 [1280], replicated, may hold values from 0.25 to 1.75
Outputs:
- input_grads: bfloat16 [64, 48, 1280], P('rep', 'tp')
- up_grads: float32 [1280, 5120], P('rep', 'tp')
- down_grads: float32 [5120, 1280], P('tp', 'rep')
- gain_grads: float32 [1280], replicated
The draws below stay inside these ranges and needn't reach their ends.
Inputs may be any that keep to these rules, and one draw needn't show every extreme that they name: `dest_rank`: the images of one index of rep go to different owners; each owner receives at most 8 images, and some owner receives exactly 8 in every draw. `dest_slot`: the images that one owner receives have distinct slots 0, 1, ... up to their count less one; other slots hold no image.
All inputs are finite; a program needn't handle non-finite values.
Results may differ from the reference program's by a relative error of at most 0.015.
Values may be sent and summed in bfloat16 or wider, within the bound.
No kernel may reach another device: no remote copies, remote signals or barrier semaphores. Data moves between devices by JAX's collectives and lax.ppermute only.
A program may use at most 128 MiB of HBM per device.

```python
import jax
import jax.numpy as jnp
from jax import lax

D = 1280
FF = 5120
PATCH = 48
IMG_DEV = 4
ENC_CAP = 8
IMAGES = 32
ENC_SLOTS = 64
N_REP = 8


def assignment(key):
    base = jax.random.fold_in(key, 4242)
    key_order, key_moves, key_source = jax.random.split(base, 3)
    half = N_REP // 2
    order = jax.random.permutation(key_order, N_REP)
    moves = jax.random.randint(key_moves, (half,), 0, IMG_DEV + 1)
    moves = moves.at[0].set(IMG_DEV)
    counts = jnp.zeros((N_REP,), jnp.int32)
    counts = counts.at[order[0::2]].add(IMG_DEV + moves)
    counts = counts.at[order[1::2]].add(IMG_DEV - moves)
    ends = jnp.cumsum(counts)
    starts = ends - counts
    entries = jnp.arange(IMG_DEV * N_REP, dtype=jnp.int32)
    owner = jnp.sum((entries[:, None] >= ends[None, :]).astype(jnp.int32), axis=1)
    position = entries - starts[owner]
    sources = jax.random.permutation(key_source, N_REP)
    source = sources[entries % N_REP]
    within = entries // N_REP
    index = source * IMG_DEV + within
    rank_out = jnp.zeros((IMG_DEV * N_REP,), jnp.int32).at[index].set(owner)
    slot_out = jnp.zeros((IMG_DEV * N_REP,), jnp.int32).at[index].set(position)
    return (rank_out, slot_out)


def draw_dest_rank(key, part):
    return assignment(key)[0]


def draw_dest_slot(key, part):
    return assignment(key)[1]


def shard_levels(own_key, dims, cuts, least, largest):
    loudness = 1.0
    for dim, shards_of in cuts:
        steps = jax.random.uniform(jax.random.fold_in(jax.random.fold_in(own_key, 6), dim), (shards_of,), jnp.float32, least / len(cuts), largest / len(cuts))
        loudness = loudness * jnp.repeat(jnp.exp(steps), dims[dim] // shards_of).reshape((-1,) + (1,) * (len(dims) - 1 - dim))
    return loudness


def gaussian(rng, dims, deviation, bound, cuts=(), held_as=jnp.bfloat16):
    loudness = shard_levels(rng, dims, cuts, -0.22, 0.18) if cuts else 1.0
    array = jax.random.normal(rng, dims, jnp.float32) * deviation * loudness
    return jnp.minimum(jnp.maximum(array, -bound), bound).astype(held_as)


def setup_inputs(seed: int = 0) -> dict:
    arg_keys = jax.random.split(jax.random.key(seed), 8)
    return {
        "image_grads": gaussian(arg_keys[0], (IMAGES, PATCH, D), 1.0, 6.0, ((0, 8), (1, 4))),
        "dest_rank": draw_dest_rank(jax.random.fold_in(arg_keys[7], 71), 0),
        "dest_slot": draw_dest_slot(jax.random.fold_in(arg_keys[7], 71), 0),
        "saved_inputs": gaussian(arg_keys[3], (ENC_SLOTS, PATCH, D), 1.0, 6.0, ((0, 8),)),
        "up_weight": gaussian(arg_keys[4], (D, FF), D ** -0.5, 0.15625, ((1, 4),)),
        "down_weight": gaussian(arg_keys[5], (FF, D), FF ** -0.5, 0.078125, ((0, 4),)),
        "norm_gain": jnp.clip(1.0 + 0.15 * jax.random.normal(arg_keys[6], (D,), jnp.float32), 0.25, 1.75),
    }


epsilon = 1e-05
gelu_c = 0.7978845608028654
gelu_a = 0.044715

def gelu_value(preact):
    inner = jnp.tanh(gelu_c * (preact + gelu_a * preact ** 3))
    return 0.5 * preact * (1.0 + inner)

def gelu_slope(preact):
    inner = jnp.tanh(gelu_c * (preact + gelu_a * preact ** 3))
    return 0.5 * (1.0 + inner) + 0.5 * preact * (1.0 - inner * inner) * gelu_c * (1.0 + 3.0 * gelu_a * preact * preact)

def reference(image_grads, dest_rank, dest_slot, saved_inputs, up_weight, down_weight, norm_gain):
    target = (dest_rank * ENC_CAP + dest_slot).astype(jnp.int32)
    routed = jnp.zeros((ENC_SLOTS, PATCH, D), jnp.bfloat16).at[target].set(image_grads)
    rows = ENC_CAP * PATCH
    saved_blocks = saved_inputs.reshape(N_REP, rows, D)
    routed_blocks = routed.reshape(N_REP, rows, D)

    def one_block(carry, pieces):
        up_acc, down_acc, gain_acc = carry
        inputs, grads = pieces
        values = inputs.astype(jnp.float32)
        mean_v = lax.optimization_barrier(jnp.mean(values, axis=1, keepdims=True))
        var_v = lax.optimization_barrier(jnp.mean((values - mean_v) ** 2, axis=1, keepdims=True))
        inv_std = 1.0 / jnp.sqrt(var_v + epsilon)
        centred = (values - mean_v) * inv_std
        normed = (centred * norm_gain[None, :]).astype(jnp.bfloat16)
        preact = jnp.dot(normed, up_weight, preferred_element_type=jnp.float32)
        hidden = gelu_value(preact).astype(jnp.bfloat16)
        grad_hidden = jnp.dot(grads, down_weight.T, preferred_element_type=jnp.float32)
        grad_pre = (grad_hidden * gelu_slope(preact)).astype(jnp.bfloat16)
        down_acc = down_acc + jnp.dot(hidden.T, grads, preferred_element_type=jnp.float32)
        up_acc = up_acc + jnp.dot(normed.T, grad_pre, preferred_element_type=jnp.float32)
        grad_normed = jnp.dot(grad_pre, up_weight.T, preferred_element_type=jnp.float32)
        gain_acc = gain_acc + lax.optimization_barrier(jnp.sum(grad_normed * centred, axis=0))
        scaled = grad_normed * norm_gain[None, :]
        first = lax.optimization_barrier(jnp.mean(scaled, axis=1, keepdims=True))
        second = lax.optimization_barrier(jnp.mean(scaled * centred, axis=1, keepdims=True))
        result = grads.astype(jnp.float32) + inv_std * (scaled - first - centred * second)
        return ((up_acc, down_acc, gain_acc), result.astype(jnp.bfloat16))
    start = (jnp.zeros((D, FF), jnp.float32), jnp.zeros((FF, D), jnp.float32), jnp.zeros((D,), jnp.float32))
    (up_grads, down_grads, gain_grads), outs = lax.scan(one_block, start, (saved_blocks, routed_blocks))
    input_grads = outs.reshape(ENC_SLOTS, PATCH, D)
    return (input_grads, up_grads, down_grads, gain_grads)
```

```python
import jax
import jax.numpy as jnp
from jax import lax
from jax.sharding import PartitionSpec as P

epsilon = 1e-05
gelu_c = 0.7978845608028654
gelu_a = 0.044715


def gelu_value(preact):
    inner = jnp.tanh(gelu_c * (preact + gelu_a * preact**3))
    return 0.5 * preact * (1.0 + inner)


def gelu_slope(preact):
    inner = jnp.tanh(gelu_c * (preact + gelu_a * preact**3))
    return 0.5 * (1.0 + inner) + 0.5 * preact * (1.0 - inner * inner) * gelu_c * (
        1.0 + 3.0 * gelu_a * preact * preact
    )


def gelu_both(preact):
    square = preact * preact
    inner = jnp.tanh(gelu_c * (preact + gelu_a * preact * square))
    half = 0.5 * (1.0 + inner)
    slope = half + 0.5 * preact * (1.0 - inner * inner) * gelu_c * (1.0 + 3.0 * gelu_a * square)
    return preact * half, slope


def matmul(a, b):
    return jnp.dot(a, b, preferred_element_type=jnp.float32)


def matmul_nt(a, b):
    return lax.dot_general(a, b, (((1,), (1,)), ((), ())), preferred_element_type=jnp.float32)


def matmul_tn(a, b):
    return lax.dot_general(a, b, (((0,), (0,)), ((), ())), preferred_element_type=jnp.float32)


def outbound(images, dest_rank, dest_slot, groups, capacity):
    rank_ids = jnp.arange(groups, dtype=jnp.int32)
    one_hot = dest_rank[None, :] == rank_ids[:, None]
    packed = jnp.einsum(
        "ek,kpd->epd", one_hot.astype(jnp.bfloat16), images, preferred_element_type=jnp.float32
    ).astype(jnp.bfloat16)
    present = jnp.any(one_hot, axis=1)
    slot_sent = jnp.sum(jnp.where(one_hot, dest_slot[None, :], 0), axis=1) + jnp.where(
        present, 0, capacity
    )
    return (packed, slot_sent)


def compact(inbound, slot_recv, capacity):
    slot_ids = jnp.arange(capacity, dtype=jnp.int32)
    picker = (slot_recv[None, :] == slot_ids[:, None]).astype(jnp.bfloat16)
    return jnp.einsum("ce,epd->cpd", picker, inbound, preferred_element_type=jnp.float32).astype(
        jnp.bfloat16
    )


def local_reduce(image_grads, dest_rank, dest_slot, saved_inputs, up_weight, down_weight, norm_gain):
    groups = lax.axis_size("rep")
    capacity = saved_inputs.shape[0]
    patches = saved_inputs.shape[1]
    width = saved_inputs.shape[2]
    slab = image_grads.shape[1]
    packed, slot_sent = outbound(image_grads, dest_rank, dest_slot, groups, capacity)
    inbound, slot_recv = (
        lax.all_to_all(packed, "rep", split_axis=0, concat_axis=0, tiled=True),
        lax.all_to_all(slot_sent, "rep", split_axis=0, concat_axis=0, tiled=True),
    )
    routed = lax.all_gather(compact(inbound, slot_recv, capacity), "tp", axis=1, tiled=True)
    rows = capacity * patches
    grads = routed.reshape(rows, width)
    values = saved_inputs.reshape(rows, width).astype(jnp.float32)
    mean_v = jnp.mean(values, axis=1, keepdims=True)
    var_v = jnp.mean((values - mean_v) ** 2, axis=1, keepdims=True)
    inv_std = 1.0 / jnp.sqrt(var_v + epsilon)
    centred = (values - mean_v) * inv_std
    normed = (centred * norm_gain[None, :]).astype(jnp.bfloat16)
    preact = jnp.dot(normed, up_weight, preferred_element_type=jnp.float32)
    hidden = gelu_value(preact).astype(jnp.bfloat16)
    grad_hidden = jnp.dot(grads, down_weight.T, preferred_element_type=jnp.float32)
    grad_pre = (grad_hidden * gelu_slope(preact)).astype(jnp.bfloat16)
    down_local = jnp.dot(hidden.T, grads, preferred_element_type=jnp.float32)
    up_local = jnp.dot(normed.T, grad_pre, preferred_element_type=jnp.float32)
    partial_normed = jnp.dot(grad_pre, up_weight.T, preferred_element_type=jnp.float32)
    up_grads, down_grads = (
        lax.psum_scatter(
            up_local.astype(jnp.bfloat16), "rep", scatter_dimension=0, tiled=True
        ).astype(jnp.float32),
        lax.psum_scatter(
            down_local.astype(jnp.bfloat16), "rep", scatter_dimension=1, tiled=True
        ).astype(jnp.float32),
    )
    start = lax.axis_index("tp") * slab
    grad_normed = lax.psum(partial_normed.astype(jnp.bfloat16), "tp").astype(jnp.float32)
    gain_grads = lax.psum(jnp.sum(grad_normed * centred, axis=0), "rep")
    scaled = grad_normed * norm_gain[None, :]
    first = jnp.mean(scaled, axis=1, keepdims=True)
    second = jnp.mean(scaled * centred, axis=1, keepdims=True)
    result = grads.astype(jnp.float32) + inv_std * (scaled - first - centred * second)
    result = result.reshape(capacity, patches, width)
    input_grads = lax.dynamic_slice_in_dim(result, start, slab, 1).astype(jnp.bfloat16)
    return (input_grads, up_grads, down_grads, gain_grads)


def shift(x, axis, amount):
    size = lax.axis_size(axis)
    return lax.ppermute(x, axis, [(i, (i + amount) % size) for i in range(size)])


def flip(x, axis, bit):
    size = lax.axis_size(axis)
    return lax.ppermute(x, axis, [(i, i ^ bit) for i in range(size)])


def spread(block):
    groups = lax.axis_size("rep")
    fars = [block] + [shift(block, "rep", 2 * k) for k in range(1, groups // 2)]
    half = len(fars) // 2
    one = jnp.concatenate(fars[:half])
    two = jnp.concatenate(fars[half:])
    one = jnp.concatenate([one, flip(one, "rep", 1)])
    two = jnp.concatenate([two, flip(two, "tp", 2)])
    one_far = flip(one, "tp", 2)
    two_far = flip(two, "rep", 1)
    mine = jnp.concatenate([one, one_far, two, two_far])
    return (mine, flip(mine, "tp", 1))


def spread_ids():
    groups = lax.axis_size("rep")
    rep = lax.axis_index("rep")
    tp = lax.axis_index("tp")
    fars = [((rep - 2 * k) % groups, tp) for k in range(groups // 2)]
    half = len(fars) // 2
    one, two = fars[:half], fars[half:]
    one = one + [(r ^ 1, t) for r, t in one]
    two = two + [(r, t ^ 2) for r, t in two]
    mine = one + [(r, t ^ 2) for r, t in one] + two + [(r ^ 1, t) for r, t in two]
    both = mine + [(r, t ^ 1) for r, t in mine]
    return jnp.stack([r for r, _ in both]), jnp.stack([t for _, t in both])


def sum_everywhere(x):
    for axis in ("tp", "rep"):
        bit = 1
        while bit < lax.axis_size(axis):
            x = x + flip(x, axis, bit)
            bit *= 2
    return x


def local_gather(image_grads, dest_rank, dest_slot, saved_inputs, up_weight, down_weight, norm_gain):
    groups = lax.axis_size("rep")
    cuts = lax.axis_size("tp")
    rep = lax.axis_index("rep")
    tp = lax.axis_index("tp")
    capacity, patches, width = saved_inputs.shape
    held, slab = image_grads.shape[:2]
    rows = capacity * patches
    share = width // groups

    slot_ids = jnp.arange(capacity, dtype=jnp.int32)
    owners = jnp.arange(groups, dtype=jnp.int32)
    goes = dest_rank[None, :] == owners[:, None]
    code = dest_slot + capacity * jnp.arange(held, dtype=jnp.int32)
    sent = jnp.sum(jnp.where(goes, code[None, :], 0), axis=1) + jnp.where(
        jnp.any(goes, axis=1), 0, capacity * held
    )
    codes = lax.all_to_all(sent, "rep", split_axis=0, concat_axis=0, tiled=True)
    from_slot = jnp.where(codes < capacity * held, codes % capacity, capacity)
    from_place = codes // capacity

    grads_all = spread(image_grads.reshape(held * slab, width))

    values = saved_inputs.reshape(rows, width).astype(jnp.float32)
    mean_v = jnp.mean(values, axis=1, keepdims=True)
    var_v = jnp.mean((values - mean_v) ** 2, axis=1, keepdims=True)
    inv_std = 1.0 / jnp.sqrt(var_v + epsilon)
    centred = (values - mean_v) * inv_std
    normed = (centred * norm_gain[None, :]).astype(jnp.bfloat16)

    mine = lax.dynamic_slice_in_dim(normed.reshape(capacity, patches, width), tp * slab, slab, 1)
    picker = (from_slot[:, None] == slot_ids[None, :]).astype(jnp.bfloat16)
    packed = jnp.einsum("ec,cpd->epd", picker, mine, preferred_element_type=jnp.float32)
    inbound = lax.all_to_all(
        packed.astype(jnp.bfloat16), "rep", split_axis=0, concat_axis=0, tiled=True
    )
    unpack = (dest_rank[:, None] == owners[None, :]).astype(jnp.bfloat16)
    block = jnp.einsum("ke,epd->kpd", unpack, inbound, preferred_element_type=jnp.float32)
    normed_all = spread(block.astype(jnp.bfloat16).reshape(held * slab, width))

    rep_of, tp_of = spread_ids()
    row_ids = jnp.arange(rows, dtype=jnp.int32)
    slot_of_row = row_ids // patches
    patch_of_row = row_ids % patches
    here = from_slot[None, :] == slot_of_row[:, None]
    source_of_row = jnp.sum(jnp.where(here, owners[None, :], 0), axis=1)
    place_of_row = jnp.sum(jnp.where(here, from_place[None, :], 0), axis=1)
    tp_of_row = patch_of_row // slab
    wanted = ((source_of_row * cuts + tp_of_row) * held + place_of_row) * slab + patch_of_row % slab
    wanted = jnp.where(jnp.any(here, axis=1), wanted, -1)
    offsets = jnp.arange(held * slab, dtype=jnp.int32)
    have = ((rep_of * cuts + tp_of)[:, None] * (held * slab) + offsets[None, :]).reshape(-1)
    select = (wanted[:, None] == have[None, :]).astype(jnp.bfloat16)
    middle = have.shape[0] // 2
    grads = (
        matmul(select[:, :middle], grads_all[0]) + matmul(select[:, middle:], grads_all[1])
    ).astype(jnp.bfloat16)

    _, slope = gelu_both(matmul(normed, up_weight))
    grad_pre = (matmul_nt(grads, down_weight) * slope).astype(jnp.bfloat16)
    partial_normed = matmul_nt(grad_pre, up_weight)
    gain_grads = sum_everywhere(jnp.sum(partial_normed * centred, axis=0))
    pieces = partial_normed.reshape(capacity, cuts // 2, 2, slab, width)
    core = tp % 2
    across = tp // 2
    near = lax.dynamic_index_in_dim(pieces, core, 2, False)
    away = lax.dynamic_index_in_dim(pieces, 1 - core, 2, False).astype(jnp.bfloat16)
    near = near + flip(away, "tp", 1).astype(jnp.float32)
    far = lax.dynamic_index_in_dim(near, 1 - across, 1, False).astype(jnp.bfloat16)
    total = lax.dynamic_index_in_dim(near, across, 1, False)
    total = total + flip(far, "tp", 2).astype(jnp.float32)

    def own(x):
        x = x.reshape(capacity, patches, x.shape[-1])
        return lax.dynamic_slice_in_dim(x, tp * slab, slab, 1)

    centred_own = own(centred)
    scaled = total * norm_gain
    first = jnp.mean(scaled, axis=-1, keepdims=True)
    second = jnp.mean(scaled * centred_own, axis=-1, keepdims=True)
    input_grads = (
        own(grads).astype(jnp.float32) + own(inv_std) * (scaled - first - centred_own * second)
    ).astype(jnp.bfloat16)

    up_grads = down_grads = 0.0
    for n_rows, g_rows in zip(normed_all, grads_all):
        value, slope = gelu_both(matmul(n_rows, up_weight))
        grad_pre = (matmul_nt(g_rows, down_weight) * slope).astype(jnp.bfloat16)
        hidden = value.astype(jnp.bfloat16)
        up_grads += matmul_tn(lax.dynamic_slice_in_dim(n_rows, rep * share, share, 1), grad_pre)
        down_grads += matmul_tn(hidden, lax.dynamic_slice_in_dim(g_rows, rep * share, share, 1))
    return (input_grads, up_grads, down_grads, gain_grads)


def solution(mesh):
    groups, cuts = mesh.shape["rep"], mesh.shape["tp"]

    def local(*args):
        image_grads, _, _, _, up_weight, _, _ = args
        all_rows = image_grads.shape[0] * image_grads.shape[1] * groups * cuts
        small = all_rows <= 2 * up_weight.shape[1] and cuts == 4 and groups in (4, 8, 16)
        return (local_gather if small else local_reduce)(*args)

    in_specs = (
        P("rep", "tp", None),
        P("rep"),
        P("rep"),
        P("rep", None, None),
        P(None, "tp"),
        P("tp", None),
        P(),
    )
    out_specs = (P("rep", "tp", None), P("rep", "tp"), P("tp", "rep"), P())
    return jax.shard_map(local, mesh=mesh, in_specs=in_specs, out_specs=out_specs, check_vma=False)
```

```python
import functools
import math

import jax
import jax.numpy as jnp
import numpy as np
from jax import lax
from jax.experimental import pallas as pl
from jax.experimental.pallas import tpu as pltpu
from jax.sharding import PartitionSpec as P

epsilon = 1e-05
gelu_c = 0.7978845608028654
gelu_a = 0.044715


def gelu_value(preact):
    inner = jnp.tanh(gelu_c * (preact + gelu_a * preact**3))
    return 0.5 * preact * (1.0 + inner)


def gelu_slope(preact):
    inner = jnp.tanh(gelu_c * (preact + gelu_a * preact**3))
    return 0.5 * (1.0 + inner) + 0.5 * preact * (1.0 - inner * inner) * gelu_c * (
        1.0 + 3.0 * gelu_a * preact * preact
    )


def gelu_both(preact):
    square = preact * preact
    inner = jnp.tanh(gelu_c * (preact + gelu_a * preact * square))
    half = 0.5 * (1.0 + inner)
    slope = half + 0.5 * preact * (1.0 - inner * inner) * gelu_c * (1.0 + 3.0 * gelu_a * square)
    return preact * half, slope


def matmul(a, b):
    return jnp.dot(a, b, preferred_element_type=jnp.float32)


def matmul_nt(a, b):
    return lax.dot_general(a, b, (((1,), (1,)), ((), ())), preferred_element_type=jnp.float32)


def matmul_tn(a, b):
    return lax.dot_general(a, b, (((0,), (0,)), ((), ())), preferred_element_type=jnp.float32)


def outbound(images, dest_rank, dest_slot, groups, capacity):
    rank_ids = jnp.arange(groups, dtype=jnp.int32)
    one_hot = dest_rank[None, :] == rank_ids[:, None]
    packed = jnp.einsum(
        "ek,kpd->epd", one_hot.astype(jnp.bfloat16), images, preferred_element_type=jnp.float32
    ).astype(jnp.bfloat16)
    present = jnp.any(one_hot, axis=1)
    slot_sent = jnp.sum(jnp.where(one_hot, dest_slot[None, :], 0), axis=1) + jnp.where(
        present, 0, capacity
    )
    return (packed, slot_sent)


def compact(inbound, slot_recv, capacity):
    slot_ids = jnp.arange(capacity, dtype=jnp.int32)
    picker = (slot_recv[None, :] == slot_ids[:, None]).astype(jnp.bfloat16)
    return jnp.einsum("ce,epd->cpd", picker, inbound, preferred_element_type=jnp.float32).astype(
        jnp.bfloat16
    )


def local_reduce(image_grads, dest_rank, dest_slot, saved_inputs, up_weight, down_weight, norm_gain):
    groups = lax.axis_size("rep")
    capacity = saved_inputs.shape[0]
    patches = saved_inputs.shape[1]
    width = saved_inputs.shape[2]
    slab = image_grads.shape[1]
    packed, slot_sent = outbound(image_grads, dest_rank, dest_slot, groups, capacity)
    inbound, slot_recv = (
        lax.all_to_all(packed, "rep", split_axis=0, concat_axis=0, tiled=True),
        lax.all_to_all(slot_sent, "rep", split_axis=0, concat_axis=0, tiled=True),
    )
    routed = lax.all_gather(compact(inbound, slot_recv, capacity), "tp", axis=1, tiled=True)
    rows = capacity * patches
    grads = routed.reshape(rows, width)
    values = saved_inputs.reshape(rows, width).astype(jnp.float32)
    mean_v = jnp.mean(values, axis=1, keepdims=True)
    var_v = jnp.mean((values - mean_v) ** 2, axis=1, keepdims=True)
    inv_std = 1.0 / jnp.sqrt(var_v + epsilon)
    centred = (values - mean_v) * inv_std
    normed = (centred * norm_gain[None, :]).astype(jnp.bfloat16)
    preact = jnp.dot(normed, up_weight, preferred_element_type=jnp.float32)
    hidden = gelu_value(preact).astype(jnp.bfloat16)
    grad_hidden = jnp.dot(grads, down_weight.T, preferred_element_type=jnp.float32)
    grad_pre = (grad_hidden * gelu_slope(preact)).astype(jnp.bfloat16)
    down_local = jnp.dot(hidden.T, grads, preferred_element_type=jnp.float32)
    up_local = jnp.dot(normed.T, grad_pre, preferred_element_type=jnp.float32)
    partial_normed = jnp.dot(grad_pre, up_weight.T, preferred_element_type=jnp.float32)
    up_grads, down_grads = (
        lax.psum_scatter(
            up_local.astype(jnp.bfloat16), "rep", scatter_dimension=0, tiled=True
        ).astype(jnp.float32),
        lax.psum_scatter(
            down_local.astype(jnp.bfloat16), "rep", scatter_dimension=1, tiled=True
        ).astype(jnp.float32),
    )
    start = lax.axis_index("tp") * slab
    grad_normed = lax.psum(partial_normed.astype(jnp.bfloat16), "tp").astype(jnp.float32)
    gain_grads = lax.psum(jnp.sum(grad_normed * centred, axis=0), "rep")
    scaled = grad_normed * norm_gain[None, :]
    first = jnp.mean(scaled, axis=1, keepdims=True)
    second = jnp.mean(scaled * centred, axis=1, keepdims=True)
    result = grads.astype(jnp.float32) + inv_std * (scaled - first - centred * second)
    result = result.reshape(capacity, patches, width)
    input_grads = lax.dynamic_slice_in_dim(result, start, slab, 1).astype(jnp.bfloat16)
    return (input_grads, up_grads, down_grads, gain_grads)


LANES = 128
TILE = 256
PAD = 16
VMEM = 67_043_328


def flip(x, axis, bit):
    size = lax.axis_size(axis)
    return lax.ppermute(x, axis, [(i, i ^ bit) for i in range(size)])


def flip_both(x, rep_bit, tp_bit):
    groups, cuts = lax.axis_size("rep"), lax.axis_size("tp")
    mask = rep_bit * cuts + tp_bit
    return lax.ppermute(x, ("rep", "tp"), [(i, i ^ mask) for i in range(groups * cuts)])


def after(x, *others):
    return lax.optimization_barrier((x,) + others)[0]


def spread_far(block):
    groups = lax.axis_size("rep")
    return [block] + [flip(block, "rep", 2 * k) for k in range(1, groups // 2)]


def spread_plane(here):
    return [here, flip(here, "tp", 2), flip(here, "rep", 1), flip_both(here, 1, 2)]


def spread_core(pieces):
    return [x for piece in pieces for x in (piece, flip(piece, "tp", 1))]


def quotient(x, divisor, count):
    return sum([(x >= divisor * k).astype(jnp.int32) for k in range(1, count)], jnp.zeros_like(x))


def own_places(rows, capacity, slab):
    row = lax.broadcasted_iota(jnp.int32, (rows, 1), 0)
    part = quotient(row, capacity * slab, 4)
    row = row - part * (capacity * slab)
    patch = quotient(row, capacity, slab)
    turn = part + (part == 1).astype(jnp.int32) - (part == 2).astype(jnp.int32)
    return turn, patch, row - patch * capacity


def layer_norm(values):
    mean_v = jnp.mean(values, axis=1, keepdims=True)
    var_v = jnp.mean((values - mean_v) ** 2, axis=1, keepdims=True)
    inv_std = 1.0 / jnp.sqrt(var_v + epsilon)
    return (values - mean_v) * inv_std, inv_std


def one_hot(index, width):
    places = lax.broadcasted_iota(jnp.int32, (index.shape[0], width), 1)
    return jnp.where(index == places, 1.0, 0.0).astype(jnp.bfloat16)


SCALARS = pl.BlockSpec(memory_space=pltpu.SMEM)
FULL = pltpu.CompilerParams(vmem_limit_bytes=VMEM)


def codes_kernel(held, capacity, rank_ref, slot_ref, o_ref):
    for e in range(o_ref.shape[0]):
        code = 0
        for k in range(held):
            code += jnp.where(rank_ref[k] == e, 1 + slot_ref[k] + capacity * k, 0)
        o_ref[e] = jnp.full((1, LANES), code, jnp.int32)


def codes_sent(dest_rank, dest_slot, groups, capacity):
    return pl.pallas_call(
        functools.partial(codes_kernel, dest_rank.shape[0], capacity),
        in_specs=[SCALARS, SCALARS],
        out_shape=jax.ShapeDtypeStruct((groups, 1, LANES), jnp.int32),
        compiler_params=FULL,
    )(dest_rank, dest_slot)


def norm_kernel(slab, saved_ref, gain_ref, values_ref, normed_ref):
    capacity, patches, width = saved_ref.shape
    rows = capacity * patches
    turn, patch, slot = own_places(rows, capacity, slab)
    cut = jnp.bitwise_xor(turn, lax.axis_index("tp").astype(jnp.int32))
    saved = saved_ref[...].reshape(rows, width)
    values = matmul(one_hot(slot * patches + cut * slab + patch, rows), saved)
    values_ref[...] = values.astype(jnp.bfloat16)
    centred, _ = layer_norm(values)
    normed_ref[...] = (centred * gain_ref[...][None, :]).astype(jnp.bfloat16)


def norm_rows(saved, gain, slab):
    capacity, patches, width = saved.shape
    shape = jax.ShapeDtypeStruct((capacity * patches, width), jnp.bfloat16)
    return pl.pallas_call(
        functools.partial(norm_kernel, slab), out_shape=(shape, shape), compiler_params=FULL
    )(saved, gain)


def pack_kernel(slab, capacity, codes_ref, x_ref, o_ref):
    rows = x_ref.shape[0]
    groups = o_ref.shape[0] // PAD
    patch = lax.broadcasted_iota(jnp.int32, (PAD, rows), 0)
    place = lax.broadcasted_iota(jnp.int32, (PAD, rows), 1) - patch * capacity
    place = jnp.where(patch < slab, place, -1)
    picks = []
    for e in range(groups):
        code = codes_ref[e, 0, 0]
        slot = jnp.where(code > 0, lax.rem(code - 1, capacity), capacity)
        picks.append(jnp.where(place == slot, 1.0, 0.0))
    picks = jnp.concatenate(picks).astype(jnp.bfloat16)
    o_ref[...] = matmul(picks, x_ref[...]).astype(o_ref.dtype)


def pack(codes, normed, slab, capacity):
    groups = codes.shape[0]
    width = normed.shape[1]
    rows = slab * capacity
    return pl.pallas_call(
        functools.partial(pack_kernel, slab, capacity),
        grid=(1,),
        in_specs=[SCALARS, pl.BlockSpec((rows, width), lambda i: (0, 0))],
        out_specs=pl.BlockSpec((groups * PAD, width), lambda i: (0, 0)),
        out_shape=jax.ShapeDtypeStruct((groups * PAD, width), normed.dtype),
        compiler_params=FULL,
    )(codes, normed)


def unpack_kernel(held, slab, rank_ref, x_ref, o_ref):
    row = lax.broadcasted_iota(jnp.int32, (held * slab, 1), 0)
    patch = quotient(row, held, slab)
    image = row - patch * held
    index = patch
    for k in range(held):
        index = index + jnp.where(image == k, rank_ref[k] * PAD, 0)
    o_ref[...] = matmul(one_hot(index, x_ref.shape[0]), x_ref[...]).astype(o_ref.dtype)


def unpack(dest_rank, inbound, held, slab):
    return pl.pallas_call(
        functools.partial(unpack_kernel, held, slab),
        in_specs=[SCALARS, pl.BlockSpec(memory_space=pltpu.VMEM)],
        out_shape=jax.ShapeDtypeStruct((held * slab, inbound.shape[1]), inbound.dtype),
        compiler_params=FULL,
    )(dest_rank, inbound)


def own_index(codes_ref, rows, capacity, held, slab):
    groups = codes_ref.shape[0]
    turn, patch, slot = own_places(rows, capacity, slab)
    block = held * slab
    fars = groups // 2
    rep = lax.axis_index("rep").astype(jnp.int32)
    core = jnp.bitwise_and(turn, 1)
    across = jnp.right_shift(turn, 1)
    index = jnp.full((rows, 1), -1, jnp.int32)
    base = (across * 2 + core) * (fars * block) + patch * held
    for e in range(groups):
        code = codes_ref[e, 0, 0]
        owned = jnp.where(code > 0, lax.rem(code - 1, capacity), -1)
        image = lax.div(jnp.maximum(code - 1, 0), capacity)
        away = jnp.bitwise_xor(rep, e)
        near = jnp.bitwise_and(away, 1)
        far = jnp.right_shift(away, 1)
        index = jnp.where(slot == owned, base + near * (4 * fars * block) + far * block + image, index)
    return index


def own_kernel(count, held, slab, *refs):
    codes_ref, values_ref, normed_ref = refs[:3]
    pieces = refs[3 : 3 + count]
    up_ref, down_ref, keep_ref, away_ref, grads_ref, gain_ref, total = refs[3 + count :]
    step = pl.program_id(0)

    @pl.when(step == 0)
    def _():
        rows = values_ref.shape[0]
        index = own_index(codes_ref, rows, rows // (4 * slab), held, slab)
        grads = 0.0
        size = pieces[0].shape[0]
        for k, piece in enumerate(pieces):
            grads += matmul(one_hot(index - k * size, size), piece[...])
        grads_ref[...] = grads.astype(jnp.bfloat16)
        total[...] = jnp.zeros_like(total)

    up = up_ref[...]
    _, slope = gelu_both(matmul(normed_ref[...], up))
    grad_pre = (matmul_nt(grads_ref[...], down_ref[...]) * slope).astype(jnp.bfloat16)
    total[...] += matmul_nt(grad_pre, up)

    @pl.when(step == pl.num_programs(0) - 1)
    def _():
        centred, _ = layer_norm(values_ref[...].astype(jnp.float32))
        gain_ref[...] = jnp.sum(total[...] * centred, axis=0, keepdims=True)
        half = keep_ref.shape[0]
        keep_ref[...] = total[:half, :]
        away_ref[...] = total[half:, :].astype(jnp.bfloat16)


def own_rows(codes, values, normed, pieces, up_weight, down_weight, held, slab):
    rows, width = values.shape
    hidden = up_weight.shape[1]
    tile = min(TILE, hidden)
    whole = lambda x: pl.BlockSpec(x.shape, lambda i: (0, 0))
    size = pieces[0].shape[0] * len(pieces)
    return pl.pallas_call(
        functools.partial(own_kernel, len(pieces), held, slab),
        grid=(hidden // tile,),
        in_specs=[SCALARS, whole(values), whole(normed)]
        + [whole(x) for x in pieces]
        + [
            pl.BlockSpec((width, tile), lambda i: (0, i)),
            pl.BlockSpec((tile, width), lambda i: (i, 0)),
        ],
        out_specs=[
            pl.BlockSpec((rows // 2, width), lambda i: (0, 0)),
            pl.BlockSpec((rows // 2, width), lambda i: (0, 0)),
            pl.BlockSpec((rows, width), lambda i: (0, 0)),
            pl.BlockSpec((1, width), lambda i: (0, 0)),
        ],
        out_shape=[
            jax.ShapeDtypeStruct((rows // 2, width), jnp.float32),
            jax.ShapeDtypeStruct((rows // 2, width), jnp.bfloat16),
            jax.ShapeDtypeStruct((rows, width), jnp.bfloat16),
            jax.ShapeDtypeStruct((1, width), jnp.float32),
        ],
        scratch_shapes=[pltpu.VMEM((rows, width), jnp.float32)],
        compiler_params=FULL,
        cost_estimate=pl.CostEstimate(
            flops=2 * rows * width * (3 * hidden + size),
            bytes_accessed=2 * width * (2 * hidden + size + 4 * rows),
            transcendentals=rows * hidden,
        ),
    )(codes, values, normed, *pieces, up_weight, down_weight)


def weights_kernel(count, first, *refs):
    n_refs, g_refs = refs[:count], refs[count : 2 * count]
    up_ref, down_ref = refs[2 * count : 2 * count + 2]
    rest = refs[2 * count + 2 :]
    if not first:
        up_in, down_in = rest[:2]
        rest = rest[2:]
    up_out, down_out, n_all, g_all, wide = rest
    size = n_refs[0].shape[0]
    width = n_refs[0].shape[1]
    share = up_out.shape[0]
    window = wide.shape[0]

    @pl.when(pl.program_id(0) == 0)
    def _():
        for k in range(count):
            n_all[k * size : (k + 1) * size, :] = n_refs[k][...]
            g_all[k * size : (k + 1) * size, :] = g_refs[k][...]

    value, slope = gelu_both(matmul(n_all[...], up_ref[...]))
    grad_pre = (matmul_nt(g_all[...], down_ref[...]) * slope).astype(jnp.bfloat16)
    start = lax.axis_index("rep").astype(jnp.int32) * share
    base = jnp.minimum(lax.div(start, LANES) * LANES, width - window)
    lanes = pl.ds(pl.multiple_of(base, LANES), window)
    picked = pl.ds(pl.multiple_of(start - base, 8), share)
    wide[...] = matmul_tn(n_all[:, lanes], grad_pre)
    up = wide[picked, :]
    if not first:
        up = up + up_in[...]
    up_out[...] = up
    wide[...] = matmul_tn(g_all[:, lanes], value.astype(jnp.bfloat16))
    down = wide[picked, :]
    if not first:
        down = down + down_in[...]
    down_out[...] = down


def weight_grads(window, n_pieces, g_pieces, up_weight, down_weight, share, before):
    size, width = n_pieces[0].shape
    count = len(n_pieces)
    rows = size * count
    hidden = up_weight.shape[1]
    tile = min(TILE, hidden)
    whole = lambda x: pl.BlockSpec(x.shape, lambda i: (0, 0))
    sum_spec = pl.BlockSpec((share, tile), lambda i: (0, i))
    pieces = list(n_pieces) + list(g_pieces)
    return pl.pallas_call(
        functools.partial(weights_kernel, count, before is None),
        grid=(hidden // tile,),
        in_specs=[whole(x) for x in pieces]
        + [
            pl.BlockSpec((width, tile), lambda i: (0, i)),
            pl.BlockSpec((tile, width), lambda i: (i, 0)),
        ]
        + ([] if before is None else [sum_spec, sum_spec]),
        out_specs=[sum_spec, sum_spec],
        scratch_shapes=[
            pltpu.VMEM((rows, width), jnp.bfloat16),
            pltpu.VMEM((rows, width), jnp.bfloat16),
            pltpu.VMEM((window, tile), jnp.float32),
        ],
        out_shape=[jax.ShapeDtypeStruct((share, hidden), jnp.float32)] * 2,
        compiler_params=FULL,
        cost_estimate=pl.CostEstimate(
            flops=4 * rows * hidden * (width + window),
            bytes_accessed=4 * width * (hidden + rows) + 16 * share * hidden,
            transcendentals=rows * hidden,
        ),
    )(*pieces, up_weight, down_weight, *(before or ()))


def near_kernel(keep_ref, got_ref, near_ref, far_ref):
    half = near_ref.shape[0]
    got = got_ref[...].astype(jnp.float32)
    near_ref[...] = keep_ref[:half, :] + got[:half, :]
    far_ref[...] = (keep_ref[half:, :] + got[half:, :]).astype(jnp.bfloat16)


def add_near(keep, got):
    rows, width = keep.shape
    return pl.pallas_call(
        near_kernel,
        out_shape=(
            jax.ShapeDtypeStruct((rows // 2, width), jnp.float32),
            jax.ShapeDtypeStruct((rows // 2, width), jnp.bfloat16),
        ),
        compiler_params=FULL,
    )(keep, got)


def finish_kernel(near_ref, far_ref, values_ref, grads_ref, gain_ref, o_ref):
    centred, inv_std = layer_norm(values_ref[...].astype(jnp.float32))
    scaled = (near_ref[...] + far_ref[...].astype(jnp.float32)) * gain_ref[...][None, :]
    first = jnp.mean(scaled, axis=1, keepdims=True)
    second = jnp.mean(scaled * centred, axis=1, keepdims=True)
    result = grads_ref[...].astype(jnp.float32) + inv_std * (scaled - first - centred * second)
    o_ref[...] = result.astype(o_ref.dtype)


def finish(near, far, values, grads, gain):
    rows, width = near.shape
    top = pl.BlockSpec((rows, width), lambda i: (0, 0))
    return pl.pallas_call(
        finish_kernel,
        grid=(1,),
        in_specs=[top, top, top, top, pl.BlockSpec((width,), lambda i: (0,))],
        out_specs=top,
        out_shape=jax.ShapeDtypeStruct((rows, width), jnp.bfloat16),
        compiler_params=FULL,
    )(near, far, values, grads, gain)


def local_gather(image_grads, dest_rank, dest_slot, saved_inputs, up_weight, down_weight, norm_gain):
    groups = lax.axis_size("rep")
    capacity, _, width = saved_inputs.shape
    held, slab = image_grads.shape[:2]
    share = width // groups

    sent = codes_sent(dest_rank, dest_slot, groups, capacity)
    codes = lax.all_to_all(sent, "rep", split_axis=0, concat_axis=0, tiled=True)

    values, normed = norm_rows(saved_inputs, norm_gain, slab)
    block = after(image_grads, normed).transpose(1, 0, 2).reshape(slab * held, width)
    g_far = spread_far(block)

    codes = after(codes, normed)
    packed = pack(codes, normed, slab, capacity)
    inbound = lax.all_to_all(
        packed.reshape(groups, PAD, width), "rep", split_axis=0, concat_axis=0, tiled=True
    )
    g_plane = spread_plane(jnp.concatenate([after(g_far[0], packed)] + g_far[1:]))
    block = unpack(dest_rank, inbound.reshape(groups * PAD, width), held, slab)

    n_far = spread_far(block)
    here = jnp.concatenate(n_far)
    g_pieces = spread_core([after(piece, here) for piece in g_plane])
    n_plane = spread_plane(here)
    n_pieces = spread_core(n_plane)

    keep, away, grads, gain_part = own_rows(
        codes, values, after(normed, here), g_pieces, up_weight, down_weight, held, slab
    )

    cut = [gain_part] + [flip(gain_part, "tp", k) for k in range(1, 4)]
    gain_part = (cut[0] + cut[1]) + (cut[2] + cut[3])
    near, far = add_near(keep, flip(away, "tp", 1))
    far = flip(far, "tp", 2)

    step = math.gcd(share, LANES)
    window = min(width, -(-(share + LANES - step) // LANES) * LANES)
    sums = None
    bit = 1
    for lo, hi in CALLS:
        moved = flip(gain_part, "rep", bit)
        sums = weight_grads(
            window, n_pieces[lo:hi], g_pieces[lo:hi], up_weight, down_weight, share, sums
        )
        gain_part = gain_part + after(moved, sums[0])
        bit *= 2
    up_grads, down_grads = sums
    while bit < groups:
        gain_part = gain_part + flip(gain_part, "rep", bit)
        bit *= 2

    rows_out = finish(near, after(far, up_grads), values, grads, norm_gain)
    input_grads = rows_out.reshape(slab, capacity, width).transpose(1, 0, 2)
    return (input_grads, up_grads, down_grads.T, gain_part[0])


CALLS = ((0, 2), (2, 8))


def solution(mesh):
    groups, cuts = mesh.shape["rep"], mesh.shape["tp"]

    def local(*args):
        image_grads, _, _, _, up_weight, _, _ = args
        all_rows = image_grads.shape[0] * image_grads.shape[1] * groups * cuts
        small = all_rows <= 2 * up_weight.shape[1] and cuts == 4 and groups in (4, 8, 16)
        return (local_gather if small else local_reduce)(*args)

    in_specs = (
        P("rep", "tp", None),
        P("rep"),
        P("rep"),
        P("rep", None, None),
        P(None, "tp"),
        P("tp", None),
        P(),
    )
    out_specs = (P("rep", "tp", None), P("rep", "tp"), P("tp", "rep"), P())
    return jax.shard_map(local, mesh=mesh, in_specs=in_specs, out_specs=out_specs, check_vma=False)
```

```python
import functools
import math

import jax
import jax.numpy as jnp
from jax import lax
from jax.experimental import pallas as pl
from jax.experimental.pallas import tpu as pltpu
from jax.sharding import PartitionSpec as P


epsilon = 1e-05
gelu_c = 0.7978845608028654
gelu_a = 0.044715


def gelu_value(preact):
    inner = jnp.tanh(gelu_c * (preact + gelu_a * preact**3))
    return 0.5 * preact * (1.0 + inner)


def gelu_slope(preact):
    inner = jnp.tanh(gelu_c * (preact + gelu_a * preact**3))
    return 0.5 * (1.0 + inner) + 0.5 * preact * (1.0 - inner * inner) * gelu_c * (
        1.0 + 3.0 * gelu_a * preact * preact
    )


def gelu_both(preact):
    square = preact * preact
    inner = jnp.tanh(gelu_c * (preact + gelu_a * preact * square))
    half = 0.5 * (1.0 + inner)
    slope = half + 0.5 * preact * (1.0 - inner * inner) * gelu_c * (1.0 + 3.0 * gelu_a * square)
    return preact * half, slope


def matmul(a, b):
    return jnp.dot(a, b, preferred_element_type=jnp.float32)


def matmul_nt(a, b):
    return lax.dot_general(a, b, (((1,), (1,)), ((), ())), preferred_element_type=jnp.float32)


def matmul_tn(a, b):
    return lax.dot_general(a, b, (((0,), (0,)), ((), ())), preferred_element_type=jnp.float32)


def outbound(images, dest_rank, dest_slot, groups, capacity):
    rank_ids = jnp.arange(groups, dtype=jnp.int32)
    one_hot = dest_rank[None, :] == rank_ids[:, None]
    packed = jnp.einsum(
        "ek,kpd->epd", one_hot.astype(jnp.bfloat16), images, preferred_element_type=jnp.float32
    ).astype(jnp.bfloat16)
    present = jnp.any(one_hot, axis=1)
    slot_sent = jnp.sum(jnp.where(one_hot, dest_slot[None, :], 0), axis=1) + jnp.where(
        present, 0, capacity
    )
    return (packed, slot_sent)


def compact(inbound, slot_recv, capacity):
    slot_ids = jnp.arange(capacity, dtype=jnp.int32)
    picker = (slot_recv[None, :] == slot_ids[:, None]).astype(jnp.bfloat16)
    return jnp.einsum("ce,epd->cpd", picker, inbound, preferred_element_type=jnp.float32).astype(
        jnp.bfloat16
    )


def local_reduce(image_grads, dest_rank, dest_slot, saved_inputs, up_weight, down_weight, norm_gain):
    groups = lax.axis_size("rep")
    capacity = saved_inputs.shape[0]
    patches = saved_inputs.shape[1]
    width = saved_inputs.shape[2]
    slab = image_grads.shape[1]
    packed, slot_sent = outbound(image_grads, dest_rank, dest_slot, groups, capacity)
    inbound, slot_recv = (
        lax.all_to_all(packed, "rep", split_axis=0, concat_axis=0, tiled=True),
        lax.all_to_all(slot_sent, "rep", split_axis=0, concat_axis=0, tiled=True),
    )
    routed = lax.all_gather(compact(inbound, slot_recv, capacity), "tp", axis=1, tiled=True)
    rows = capacity * patches
    grads = routed.reshape(rows, width)
    values = saved_inputs.reshape(rows, width).astype(jnp.float32)
    mean_v = jnp.mean(values, axis=1, keepdims=True)
    var_v = jnp.mean((values - mean_v) ** 2, axis=1, keepdims=True)
    inv_std = 1.0 / jnp.sqrt(var_v + epsilon)
    centred = (values - mean_v) * inv_std
    normed = (centred * norm_gain[None, :]).astype(jnp.bfloat16)
    preact = jnp.dot(normed, up_weight, preferred_element_type=jnp.float32)
    hidden = gelu_value(preact).astype(jnp.bfloat16)
    grad_hidden = jnp.dot(grads, down_weight.T, preferred_element_type=jnp.float32)
    grad_pre = (grad_hidden * gelu_slope(preact)).astype(jnp.bfloat16)
    down_local = jnp.dot(hidden.T, grads, preferred_element_type=jnp.float32)
    up_local = jnp.dot(normed.T, grad_pre, preferred_element_type=jnp.float32)
    partial_normed = jnp.dot(grad_pre, up_weight.T, preferred_element_type=jnp.float32)
    up_grads, down_grads = (
        lax.psum_scatter(
            up_local.astype(jnp.bfloat16), "rep", scatter_dimension=0, tiled=True
        ).astype(jnp.float32),
        lax.psum_scatter(
            down_local.astype(jnp.bfloat16), "rep", scatter_dimension=1, tiled=True
        ).astype(jnp.float32),
    )
    start = lax.axis_index("tp") * slab
    grad_normed = lax.psum(partial_normed.astype(jnp.bfloat16), "tp").astype(jnp.float32)
    gain_grads = lax.psum(jnp.sum(grad_normed * centred, axis=0), "rep")
    scaled = grad_normed * norm_gain[None, :]
    first = jnp.mean(scaled, axis=1, keepdims=True)
    second = jnp.mean(scaled * centred, axis=1, keepdims=True)
    result = grads.astype(jnp.float32) + inv_std * (scaled - first - centred * second)
    result = result.reshape(capacity, patches, width)
    input_grads = lax.dynamic_slice_in_dim(result, start, slab, 1).astype(jnp.bfloat16)
    return (input_grads, up_grads, down_grads, gain_grads)


LANES = 128
TILE = 256
PAD = 16
VMEM = 40_000_000
FULL = pltpu.CompilerParams(vmem_limit_bytes=VMEM)
SCALARS = pl.BlockSpec(memory_space=pltpu.SMEM)
ANYWHERE = pl.BlockSpec(memory_space=pl.ANY)


def flip(x, axis, bit):
    size = lax.axis_size(axis)
    return lax.ppermute(x, axis, [(i, i ^ bit) for i in range(size)])


def flip_both(x, rep_bit, tp_bit):
    groups, cuts = lax.axis_size("rep"), lax.axis_size("tp")
    mask = rep_bit * cuts + tp_bit
    return lax.ppermute(x, ("rep", "tp"), [(i, i ^ mask) for i in range(groups * cuts)])


def after(x, *others):
    return lax.optimization_barrier((x,) + others)[0]


def spread_far(block):
    groups = lax.axis_size("rep")
    return [block] + [flip(block, "rep", 2 * k) for k in range(1, groups // 2)]


def spread_plane(here):
    return [here, flip(here, "tp", 2), flip(here, "rep", 1), flip_both(here, 1, 2)]


def spread_core(pieces):
    return [x for piece in pieces for x in (piece, flip(piece, "tp", 1))]


def join_kernel(*refs):
    o_ref = refs[-1]
    size = refs[0].shape[0]
    for k, ref in enumerate(refs[:-1]):
        o_ref[k * size : (k + 1) * size, :] = ref[...]


def join(pieces):
    size, width = pieces[0].shape
    return pl.pallas_call(
        join_kernel,
        out_shape=jax.ShapeDtypeStruct((size * len(pieces), width), pieces[0].dtype),
        compiler_params=FULL,
    )(*pieces)


def quotient(x, divisor, count):
    return sum([(x >= divisor * k).astype(jnp.int32) for k in range(1, count)], jnp.zeros_like(x))


def own_places(rows, capacity, slab):
    row = lax.broadcasted_iota(jnp.int32, (rows, 1), 0)
    part = quotient(row, capacity * slab, 4)
    row = row - part * (capacity * slab)
    patch = quotient(row, capacity, slab)
    turn = part + (part == 1).astype(jnp.int32) - (part == 2).astype(jnp.int32)
    return turn, patch, row - patch * capacity


def layer_norm(values):
    mean_v = jnp.mean(values, axis=1, keepdims=True)
    var_v = jnp.mean((values - mean_v) ** 2, axis=1, keepdims=True)
    inv_std = 1.0 / jnp.sqrt(var_v + epsilon)
    return (values - mean_v) * inv_std, inv_std


def one_hot(index, width):
    places = lax.broadcasted_iota(jnp.int32, (index.shape[0], width), 1)
    return jnp.where(index == places, 1.0, 0.0).astype(jnp.bfloat16)


def copies(pieces, all_ref, sems):
    size = pieces[0].shape[0]
    return [
        pltpu.make_async_copy(piece, all_ref.at[pl.ds(k * size, size), :], sems.at[k])
        for k, piece in enumerate(pieces)
    ]


def codes_kernel(held, capacity, rank_ref, slot_ref, o_ref):
    for e in range(o_ref.shape[0]):
        code = 0
        for k in range(held):
            code += jnp.where(rank_ref[k] == e, 1 + slot_ref[k] + capacity * k, 0)
        o_ref[e] = jnp.full((1, LANES), code, jnp.int32)


def codes_sent(dest_rank, dest_slot, groups, capacity):
    return pl.pallas_call(
        functools.partial(codes_kernel, dest_rank.shape[0], capacity),
        in_specs=[SCALARS, SCALARS],
        out_shape=jax.ShapeDtypeStruct((groups, 1, LANES), jnp.int32),
        compiler_params=FULL,
    )(dest_rank, dest_slot)


def norm_kernel(slab, saved_ref, gain_ref, values_ref, normed_ref):
    capacity, patches, width = saved_ref.shape
    rows = capacity * patches
    turn, patch, slot = own_places(rows, capacity, slab)
    cut = jnp.bitwise_xor(turn, lax.axis_index("tp").astype(jnp.int32))
    saved = saved_ref[...].reshape(rows, width)
    values = matmul(one_hot(slot * patches + cut * slab + patch, rows), saved)
    values_ref[...] = values.astype(jnp.bfloat16)
    centred, _ = layer_norm(values)
    normed_ref[...] = (centred * gain_ref[...][None, :]).astype(jnp.bfloat16)


def norm_rows(saved, gain, slab):
    capacity, patches, width = saved.shape
    shape = jax.ShapeDtypeStruct((capacity * patches, width), jnp.bfloat16)
    return pl.pallas_call(
        functools.partial(norm_kernel, slab), out_shape=(shape, shape), compiler_params=FULL
    )(saved, gain)


def pack_kernel(slab, capacity, codes_ref, x_ref, o_ref):
    rows = x_ref.shape[0]
    groups = o_ref.shape[0] // PAD
    patch = lax.broadcasted_iota(jnp.int32, (PAD, rows), 0)
    place = lax.broadcasted_iota(jnp.int32, (PAD, rows), 1) - patch * capacity
    place = jnp.where(patch < slab, place, -1)
    picks = []
    for e in range(groups):
        code = codes_ref[e, 0, 0]
        slot = jnp.where(code > 0, lax.rem(code - 1, capacity), capacity)
        picks.append(jnp.where(place == slot, 1.0, 0.0))
    picks = jnp.concatenate(picks).astype(jnp.bfloat16)
    o_ref[...] = matmul(picks, x_ref[...]).astype(o_ref.dtype)


def pack(codes, normed, slab, capacity):
    groups = codes.shape[0]
    width = normed.shape[1]
    rows = slab * capacity
    return pl.pallas_call(
        functools.partial(pack_kernel, slab, capacity),
        grid=(1,),
        in_specs=[SCALARS, pl.BlockSpec((rows, width), lambda i: (0, 0))],
        out_specs=pl.BlockSpec((groups * PAD, width), lambda i: (0, 0)),
        out_shape=jax.ShapeDtypeStruct((groups * PAD, width), normed.dtype),
        compiler_params=FULL,
    )(codes, normed)


def unpack_kernel(held, slab, rank_ref, x_ref, o_ref):
    row = lax.broadcasted_iota(jnp.int32, (held * slab, 1), 0)
    patch = quotient(row, held, slab)
    image = row - patch * held
    index = patch
    for k in range(held):
        index = index + jnp.where(image == k, rank_ref[k] * PAD, 0)
    o_ref[...] = matmul(one_hot(index, x_ref.shape[0]), x_ref[...]).astype(o_ref.dtype)


def unpack(dest_rank, inbound, held, slab):
    return pl.pallas_call(
        functools.partial(unpack_kernel, held, slab),
        in_specs=[SCALARS, pl.BlockSpec(memory_space=pltpu.VMEM)],
        out_shape=jax.ShapeDtypeStruct((held * slab, inbound.shape[1]), inbound.dtype),
        compiler_params=FULL,
    )(dest_rank, inbound)


def own_index(codes_ref, rows, capacity, held, slab):
    groups = codes_ref.shape[0]
    turn, patch, slot = own_places(rows, capacity, slab)
    block = held * slab
    fars = groups // 2
    rep = lax.axis_index("rep").astype(jnp.int32)
    core = jnp.bitwise_and(turn, 1)
    across = jnp.right_shift(turn, 1)
    index = jnp.full((rows, 1), -1, jnp.int32)
    base = (across * 2 + core) * (fars * block) + patch * held
    for e in range(groups):
        code = codes_ref[e, 0, 0]
        owned = jnp.where(code > 0, lax.rem(code - 1, capacity), -1)
        image = lax.div(jnp.maximum(code - 1, 0), capacity)
        away = jnp.bitwise_xor(rep, e)
        near = jnp.bitwise_and(away, 1)
        far = jnp.right_shift(away, 1)
        index = jnp.where(slot == owned, base + near * (4 * fars * block) + far * block + image, index)
    return index


def own_kernel(count, held, slab, *refs):
    codes_ref, values_ref, normed_ref = refs[:3]
    pieces = refs[3 : 3 + count]
    up_ref, down_ref, keep_ref, away_ref, grads_ref, gain_ref = refs[3 + count : 9 + count]
    total, g_all, sems = refs[9 + count :]
    step = pl.program_id(0)

    @pl.when(step == 0)
    def _():
        for copy in copies(pieces, g_all, sems):
            copy.start()

    up = up_ref[...]
    _, slope = gelu_both(matmul(normed_ref[...], up))

    @pl.when(step == 0)
    def _():
        rows = values_ref.shape[0]
        index = own_index(codes_ref, rows, rows // (4 * slab), held, slab)
        picks = one_hot(index, g_all.shape[0])
        for copy in copies(pieces, g_all, sems):
            copy.wait()
        grads_ref[...] = matmul(picks, g_all[...]).astype(jnp.bfloat16)
        total[...] = jnp.zeros_like(total)

    grad_pre = (matmul_nt(grads_ref[...], down_ref[...]) * slope).astype(jnp.bfloat16)
    total[...] += matmul_nt(grad_pre, up)

    @pl.when(step == pl.num_programs(0) - 1)
    def _():
        centred, _ = layer_norm(values_ref[...].astype(jnp.float32))
        gain_ref[...] = jnp.sum(total[...] * centred, axis=0, keepdims=True)
        half = keep_ref.shape[0]
        keep_ref[...] = total[:half, :]
        away_ref[...] = total[half:, :].astype(jnp.bfloat16)


def own_rows(codes, values, normed, pieces, up_weight, down_weight, held, slab):
    rows, width = values.shape
    hidden = up_weight.shape[1]
    tile = min(TILE, hidden)
    whole = lambda x: pl.BlockSpec(x.shape, lambda i: (0, 0))
    size = pieces[0].shape[0] * len(pieces)
    return pl.pallas_call(
        functools.partial(own_kernel, len(pieces), held, slab),
        grid=(hidden // tile,),
        in_specs=[SCALARS, whole(values), whole(normed)]
        + [ANYWHERE] * len(pieces)
        + [
            pl.BlockSpec((width, tile), lambda i: (0, i)),
            pl.BlockSpec((tile, width), lambda i: (i, 0)),
        ],
        out_specs=[
            pl.BlockSpec((rows // 2, width), lambda i: (0, 0)),
            pl.BlockSpec((rows // 2, width), lambda i: (0, 0)),
            pl.BlockSpec((rows, width), lambda i: (0, 0)),
            pl.BlockSpec((1, width), lambda i: (0, 0)),
        ],
        out_shape=[
            jax.ShapeDtypeStruct((rows // 2, width), jnp.float32),
            jax.ShapeDtypeStruct((rows // 2, width), jnp.bfloat16),
            jax.ShapeDtypeStruct((rows, width), jnp.bfloat16),
            jax.ShapeDtypeStruct((1, width), jnp.float32),
        ],
        scratch_shapes=[
            pltpu.VMEM((rows, width), jnp.float32),
            pltpu.VMEM((size, width), jnp.bfloat16),
            pltpu.SemaphoreType.DMA((len(pieces),)),
        ],
        compiler_params=FULL,
        cost_estimate=pl.CostEstimate(
            flops=2 * rows * width * (3 * hidden + size),
            bytes_accessed=2 * width * (2 * hidden + size + 4 * rows),
            transcendentals=rows * hidden,
        ),
    )(codes, values, normed, *pieces, up_weight, down_weight)


def weights_kernel(count, first, *refs):
    n_refs, g_refs = refs[:count], refs[count : 2 * count]
    up_ref, down_ref = refs[2 * count : 2 * count + 2]
    rest = refs[2 * count + 2 :]
    if not first:
        up_in, down_in = rest[:2]
        rest = rest[2:]
    up_out, down_out, n_all, g_all, wide, n_sems, g_sems = rest
    width = n_refs[0].shape[1]
    share = up_out.shape[0]
    window = wide.shape[0]

    @pl.when(pl.program_id(0) == 0)
    def _():
        moves = copies(n_refs, n_all, n_sems) + copies(g_refs, g_all, g_sems)
        for copy in moves:
            copy.start()
        for copy in moves:
            copy.wait()

    value, slope = gelu_both(matmul(n_all[...], up_ref[...]))
    grad_pre = (matmul_nt(g_all[...], down_ref[...]) * slope).astype(jnp.bfloat16)
    start = lax.axis_index("rep").astype(jnp.int32) * share
    base = jnp.minimum(lax.div(start, LANES) * LANES, width - window)
    lanes = pl.ds(pl.multiple_of(base, LANES), window)
    picked = pl.ds(pl.multiple_of(start - base, 8), share)
    wide[...] = matmul_tn(n_all[:, lanes], grad_pre)
    up = wide[picked, :]
    if not first:
        up = up + up_in[...]
    up_out[...] = up
    wide[...] = matmul_tn(g_all[:, lanes], value.astype(jnp.bfloat16))
    down = wide[picked, :]
    if not first:
        down = down + down_in[...]
    down_out[...] = down


def weight_grads(window, n_pieces, g_pieces, up_weight, down_weight, share, before):
    size, width = n_pieces[0].shape
    count = len(n_pieces)
    rows = size * count
    hidden = up_weight.shape[1]
    tile = min(TILE, hidden)
    sum_spec = pl.BlockSpec((share, tile), lambda i: (0, i))
    pieces = list(n_pieces) + list(g_pieces)
    return pl.pallas_call(
        functools.partial(weights_kernel, count, before is None),
        grid=(hidden // tile,),
        in_specs=[ANYWHERE] * len(pieces)
        + [
            pl.BlockSpec((width, tile), lambda i: (0, i)),
            pl.BlockSpec((tile, width), lambda i: (i, 0)),
        ]
        + ([] if before is None else [sum_spec, sum_spec]),
        out_specs=[sum_spec, sum_spec],
        scratch_shapes=[
            pltpu.VMEM((rows, width), jnp.bfloat16),
            pltpu.VMEM((rows, width), jnp.bfloat16),
            pltpu.VMEM((window, tile), jnp.float32),
            pltpu.SemaphoreType.DMA((count,)),
            pltpu.SemaphoreType.DMA((count,)),
        ],
        out_shape=[jax.ShapeDtypeStruct((share, hidden), jnp.float32)] * 2,
        compiler_params=FULL,
        cost_estimate=pl.CostEstimate(
            flops=4 * rows * hidden * (width + window),
            bytes_accessed=4 * width * (hidden + rows) + 16 * share * hidden,
            transcendentals=rows * hidden,
        ),
    )(*pieces, up_weight, down_weight, *(before or ()))


def near_kernel(keep_ref, got_ref, near_ref, far_ref):
    half = near_ref.shape[0]
    got = got_ref[...].astype(jnp.float32)
    near_ref[...] = keep_ref[:half, :] + got[:half, :]
    far_ref[...] = (keep_ref[half:, :] + got[half:, :]).astype(jnp.bfloat16)


def add_near(keep, got):
    rows, width = keep.shape
    return pl.pallas_call(
        near_kernel,
        out_shape=(
            jax.ShapeDtypeStruct((rows // 2, width), jnp.float32),
            jax.ShapeDtypeStruct((rows // 2, width), jnp.bfloat16),
        ),
        compiler_params=FULL,
    )(keep, got)


def finish_kernel(near_ref, far_ref, values_ref, grads_ref, gain_ref, o_ref):
    centred, inv_std = layer_norm(values_ref[...].astype(jnp.float32))
    scaled = (near_ref[...] + far_ref[...].astype(jnp.float32)) * gain_ref[...][None, :]
    first = jnp.mean(scaled, axis=1, keepdims=True)
    second = jnp.mean(scaled * centred, axis=1, keepdims=True)
    result = grads_ref[...].astype(jnp.float32) + inv_std * (scaled - first - centred * second)
    o_ref[...] = result.astype(o_ref.dtype)


def finish(near, far, values, grads, gain):
    rows, width = near.shape
    top = pl.BlockSpec((rows, width), lambda i: (0, 0))
    return pl.pallas_call(
        finish_kernel,
        grid=(1,),
        in_specs=[top, top, top, top, pl.BlockSpec((width,), lambda i: (0,))],
        out_specs=top,
        out_shape=jax.ShapeDtypeStruct((rows, width), jnp.bfloat16),
        compiler_params=FULL,
    )(near, far, values, grads, gain)


def gather_plan(image_grads, dest_rank, dest_slot, saved_inputs, up_weight, down_weight, norm_gain):
    groups = lax.axis_size("rep")
    capacity, _, width = saved_inputs.shape
    held, slab = image_grads.shape[:2]
    share = width // groups

    sent = codes_sent(dest_rank, dest_slot, groups, capacity)
    codes = lax.all_to_all(sent, "rep", split_axis=0, concat_axis=0, tiled=True)

    values, normed = norm_rows(saved_inputs, norm_gain, slab)
    block = after(image_grads, normed).transpose(1, 0, 2).reshape(slab * held, width)
    g_far = spread_far(block)

    codes = after(codes, normed)
    packed = pack(codes, normed, slab, capacity)
    inbound = lax.all_to_all(
        packed.reshape(groups, PAD, width), "rep", split_axis=0, concat_axis=0, tiled=True
    )
    here = join(g_far)
    g_plane = spread_plane(here)
    block = unpack(dest_rank, inbound.reshape(groups * PAD, width), held, slab)

    n_far = spread_far(block)
    here = join(n_far)
    n_plane = spread_plane(here)
    n_pieces = spread_core(n_plane)
    g_pieces = spread_core(g_plane)

    keep, away, grads, gain_part = own_rows(
        codes, values, normed, g_pieces, up_weight, down_weight, held, slab
    )

    cut = [gain_part] + [flip(gain_part, "tp", k) for k in range(1, 4)]
    gain_part = (cut[0] + cut[1]) + (cut[2] + cut[3])
    moved = flip(gain_part, "rep", 1)
    away = flip(away, "tp", 1)

    step = math.gcd(share, LANES)
    window = min(width, -(-(share + LANES - step) // LANES) * LANES)
    sums = None
    bit = 2
    for lo, hi in CALLS:
        sums = weight_grads(
            window, n_pieces[lo:hi], g_pieces[lo:hi], up_weight, down_weight, share, sums
        )
        if lo == 0:
            gain_part = gain_part + after(moved, sums[0])
            moved = flip(gain_part, "rep", bit)
            near, far = add_near(keep, after(away, sums[0]))
            far = flip(far, "tp", 2)
            if bit < groups // 2:
                gain_part = gain_part + after(moved, near)
                bit *= 2
                moved = flip(gain_part, "rep", bit)
    up_grads, down_grads = sums

    rows_out = finish(near, after(far, up_grads), values, grads, norm_gain)
    input_grads = rows_out.reshape(slab, capacity, width).transpose(1, 0, 2)
    gain_part = gain_part + after(moved, up_grads)
    while bit < groups // 2:
        bit *= 2
        gain_part = gain_part + flip(gain_part, "rep", bit)
    return (input_grads, up_grads, down_grads.T, gain_part[0])


CALLS = ((0, 2), (2, 8))


def solution(mesh):
    groups, cuts = mesh.shape["rep"], mesh.shape["tp"]
    in_specs = (
        P("rep", "tp", None),
        P("rep"),
        P("rep"),
        P("rep", None, None),
        P(None, "tp"),
        P("tp", None),
        P(),
    )
    out_specs = (P("rep", "tp", None), P("rep", "tp"), P("tp", "rep"), P())

    def split(local):
        return jax.shard_map(
            local, mesh=mesh, in_specs=in_specs, out_specs=out_specs, check_vma=False
        )

    gather = split(gather_plan)
    reduce = split(local_reduce)

    def run(*args):
        all_rows = args[0].shape[0] * args[0].shape[1]
        few = all_rows <= 2 * args[4].shape[1] // cuts
        return (gather if few and cuts == 4 and groups in (4, 8, 16) else reduce)(*args)

    return run
```

```python
import functools
import math

import jax
import jax.numpy as jnp
from jax import lax
from jax.experimental import pallas as pl
from jax.experimental.pallas import tpu as pltpu
from jax.sharding import PartitionSpec as P


epsilon = 1e-05
gelu_c = 0.7978845608028654
gelu_a = 0.044715


def gelu_value(preact):
    inner = jnp.tanh(gelu_c * (preact + gelu_a * preact**3))
    return 0.5 * preact * (1.0 + inner)


def gelu_slope(preact):
    inner = jnp.tanh(gelu_c * (preact + gelu_a * preact**3))
    return 0.5 * (1.0 + inner) + 0.5 * preact * (1.0 - inner * inner) * gelu_c * (
        1.0 + 3.0 * gelu_a * preact * preact
    )


def gelu_both(preact):
    square = preact * preact
    inner = jnp.tanh(gelu_c * (preact + gelu_a * preact * square))
    half = 0.5 * (1.0 + inner)
    slope = half + 0.5 * preact * (1.0 - inner * inner) * gelu_c * (1.0 + 3.0 * gelu_a * square)
    return preact * half, slope


def matmul(a, b):
    return jnp.dot(a, b, preferred_element_type=jnp.float32)


def matmul_nt(a, b):
    return lax.dot_general(a, b, (((1,), (1,)), ((), ())), preferred_element_type=jnp.float32)


def matmul_tn(a, b):
    return lax.dot_general(a, b, (((0,), (0,)), ((), ())), preferred_element_type=jnp.float32)


def outbound(images, dest_rank, dest_slot, groups, capacity):
    rank_ids = jnp.arange(groups, dtype=jnp.int32)
    one_hot = dest_rank[None, :] == rank_ids[:, None]
    packed = jnp.einsum(
        "ek,kpd->epd", one_hot.astype(jnp.bfloat16), images, preferred_element_type=jnp.float32
    ).astype(jnp.bfloat16)
    present = jnp.any(one_hot, axis=1)
    slot_sent = jnp.sum(jnp.where(one_hot, dest_slot[None, :], 0), axis=1) + jnp.where(
        present, 0, capacity
    )
    return (packed, slot_sent)


def compact(inbound, slot_recv, capacity):
    slot_ids = jnp.arange(capacity, dtype=jnp.int32)
    picker = (slot_recv[None, :] == slot_ids[:, None]).astype(jnp.bfloat16)
    return jnp.einsum("ce,epd->cpd", picker, inbound, preferred_element_type=jnp.float32).astype(
        jnp.bfloat16
    )


def local_reduce(image_grads, dest_rank, dest_slot, saved_inputs, up_weight, down_weight, norm_gain):
    groups = lax.axis_size("rep")
    capacity = saved_inputs.shape[0]
    patches = saved_inputs.shape[1]
    width = saved_inputs.shape[2]
    slab = image_grads.shape[1]
    packed, slot_sent = outbound(image_grads, dest_rank, dest_slot, groups, capacity)
    inbound, slot_recv = (
        lax.all_to_all(packed, "rep", split_axis=0, concat_axis=0, tiled=True),
        lax.all_to_all(slot_sent, "rep", split_axis=0, concat_axis=0, tiled=True),
    )
    routed = lax.all_gather(compact(inbound, slot_recv, capacity), "tp", axis=1, tiled=True)
    rows = capacity * patches
    grads = routed.reshape(rows, width)
    values = saved_inputs.reshape(rows, width).astype(jnp.float32)
    mean_v = jnp.mean(values, axis=1, keepdims=True)
    var_v = jnp.mean((values - mean_v) ** 2, axis=1, keepdims=True)
    inv_std = 1.0 / jnp.sqrt(var_v + epsilon)
    centred = (values - mean_v) * inv_std
    normed = (centred * norm_gain[None, :]).astype(jnp.bfloat16)
    preact = jnp.dot(normed, up_weight, preferred_element_type=jnp.float32)
    hidden = gelu_value(preact).astype(jnp.bfloat16)
    grad_hidden = jnp.dot(grads, down_weight.T, preferred_element_type=jnp.float32)
    grad_pre = (grad_hidden * gelu_slope(preact)).astype(jnp.bfloat16)
    down_local = jnp.dot(hidden.T, grads, preferred_element_type=jnp.float32)
    up_local = jnp.dot(normed.T, grad_pre, preferred_element_type=jnp.float32)
    partial_normed = jnp.dot(grad_pre, up_weight.T, preferred_element_type=jnp.float32)
    up_grads, down_grads = (
        lax.psum_scatter(
            up_local.astype(jnp.bfloat16), "rep", scatter_dimension=0, tiled=True
        ).astype(jnp.float32),
        lax.psum_scatter(
            down_local.astype(jnp.bfloat16), "rep", scatter_dimension=1, tiled=True
        ).astype(jnp.float32),
    )
    start = lax.axis_index("tp") * slab
    grad_normed = lax.psum(partial_normed.astype(jnp.bfloat16), "tp").astype(jnp.float32)
    gain_grads = lax.psum(jnp.sum(grad_normed * centred, axis=0), "rep")
    scaled = grad_normed * norm_gain[None, :]
    first = jnp.mean(scaled, axis=1, keepdims=True)
    second = jnp.mean(scaled * centred, axis=1, keepdims=True)
    result = grads.astype(jnp.float32) + inv_std * (scaled - first - centred * second)
    result = result.reshape(capacity, patches, width)
    input_grads = lax.dynamic_slice_in_dim(result, start, slab, 1).astype(jnp.bfloat16)
    return (input_grads, up_grads, down_grads, gain_grads)


LANES = 128
TILE = 256
PAD = 16
VMEM = 32_000_000
FULL = pltpu.CompilerParams(vmem_limit_bytes=VMEM)
SCALARS = pl.BlockSpec(memory_space=pltpu.SMEM)
ANYWHERE = pl.BlockSpec(memory_space=pl.ANY)


def flip(x, axis, bit):
    size = lax.axis_size(axis)
    return lax.ppermute(x, axis, [(i, i ^ bit) for i in range(size)])


def flip_both(x, rep_bit, tp_bit):
    groups, cuts = lax.axis_size("rep"), lax.axis_size("tp")
    mask = rep_bit * cuts + tp_bit
    return lax.ppermute(x, ("rep", "tp"), [(i, i ^ mask) for i in range(groups * cuts)])


def after(x, *others):
    return lax.optimization_barrier((x,) + others)[0]


def spread_far(block):
    groups = lax.axis_size("rep")
    return [block] + [flip(block, "rep", 2 * k) for k in range(1, groups // 2)]


def spread_plane(here):
    return [here, flip(here, "tp", 2), flip(here, "rep", 1), flip_both(here, 1, 2)]


def spread_core(pieces):
    return [x for piece in pieces for x in (piece, flip(piece, "tp", 1))]


def join_kernel(*refs):
    o_ref = refs[-1]
    size = refs[0].shape[0]
    for k, ref in enumerate(refs[:-1]):
        o_ref[k * size : (k + 1) * size, :] = ref[...]


def join(pieces):
    size, width = pieces[0].shape
    return pl.pallas_call(
        join_kernel,
        out_shape=jax.ShapeDtypeStruct((size * len(pieces), width), pieces[0].dtype),
        compiler_params=FULL,
    )(*pieces)


def quotient(x, divisor, count):
    return sum([(x >= divisor * k).astype(jnp.int32) for k in range(1, count)], jnp.zeros_like(x))


def own_places(rows, capacity, slab):
    row = lax.broadcasted_iota(jnp.int32, (rows, 1), 0)
    part = quotient(row, capacity * slab, 4)
    row = row - part * (capacity * slab)
    patch = quotient(row, capacity, slab)
    turn = part + (part == 1).astype(jnp.int32) - (part == 2).astype(jnp.int32)
    return turn, patch, row - patch * capacity


def layer_norm(values):
    mean_v = jnp.mean(values, axis=1, keepdims=True)
    var_v = jnp.mean((values - mean_v) ** 2, axis=1, keepdims=True)
    inv_std = 1.0 / jnp.sqrt(var_v + epsilon)
    return (values - mean_v) * inv_std, inv_std


def one_hot(index, width):
    places = lax.broadcasted_iota(jnp.int32, (index.shape[0], width), 1)
    return jnp.where(index == places, 1.0, 0.0).astype(jnp.bfloat16)


def copies(pieces, all_ref, sems):
    size = pieces[0].shape[0]
    return [
        pltpu.make_async_copy(piece, all_ref.at[pl.ds(k * size, size), :], sems.at[k])
        for k, piece in enumerate(pieces)
    ]


def codes_kernel(held, capacity, rank_ref, slot_ref, o_ref):
    for e in range(o_ref.shape[0]):
        code = 0
        for k in range(held):
            code += jnp.where(rank_ref[k] == e, 1 + slot_ref[k] + capacity * k, 0)
        o_ref[e] = jnp.full((1, LANES), code, jnp.int32)


def codes_sent(dest_rank, dest_slot, groups, capacity):
    return pl.pallas_call(
        functools.partial(codes_kernel, dest_rank.shape[0], capacity),
        in_specs=[SCALARS, SCALARS],
        out_shape=jax.ShapeDtypeStruct((groups, 1, LANES), jnp.int32),
        compiler_params=pltpu.CompilerParams(vmem_limit_bytes=67_043_328),
    )(dest_rank, dest_slot)


def norm_kernel(slab, saved_ref, gain_ref, values_ref, normed_ref):
    capacity, patches, width = saved_ref.shape
    rows = capacity * patches
    turn, patch, slot = own_places(rows, capacity, slab)
    cut = jnp.bitwise_xor(turn, lax.axis_index("tp").astype(jnp.int32))
    saved = saved_ref[...].reshape(rows, width)
    values = matmul(one_hot(slot * patches + cut * slab + patch, rows), saved)
    values_ref[...] = values.astype(jnp.bfloat16)
    centred, _ = layer_norm(values)
    normed_ref[...] = (centred * gain_ref[...][None, :]).astype(jnp.bfloat16)


def norm_rows(saved, gain, slab):
    capacity, patches, width = saved.shape
    shape = jax.ShapeDtypeStruct((capacity * patches, width), jnp.bfloat16)
    return pl.pallas_call(
        functools.partial(norm_kernel, slab), out_shape=(shape, shape), compiler_params=FULL
    )(saved, gain)


def pack_kernel(slab, capacity, codes_ref, x_ref, o_ref):
    rows = x_ref.shape[0]
    groups = o_ref.shape[0] // PAD
    patch = lax.broadcasted_iota(jnp.int32, (PAD, rows), 0)
    place = lax.broadcasted_iota(jnp.int32, (PAD, rows), 1) - patch * capacity
    place = jnp.where(patch < slab, place, -1)
    picks = []
    for e in range(groups):
        code = codes_ref[e, 0, 0]
        slot = jnp.where(code > 0, lax.rem(code - 1, capacity), capacity)
        picks.append(jnp.where(place == slot, 1.0, 0.0))
    picks = jnp.concatenate(picks).astype(jnp.bfloat16)
    o_ref[...] = matmul(picks, x_ref[...]).astype(o_ref.dtype)


def pack(codes, normed, slab, capacity):
    groups = codes.shape[0]
    width = normed.shape[1]
    rows = slab * capacity
    return pl.pallas_call(
        functools.partial(pack_kernel, slab, capacity),
        grid=(1,),
        in_specs=[SCALARS, pl.BlockSpec((rows, width), lambda i: (0, 0))],
        out_specs=pl.BlockSpec((groups * PAD, width), lambda i: (0, 0)),
        out_shape=jax.ShapeDtypeStruct((groups * PAD, width), normed.dtype),
        compiler_params=FULL,
    )(codes, normed)


def unpack_kernel(held, slab, rank_ref, x_ref, o_ref):
    row = lax.broadcasted_iota(jnp.int32, (held * slab, 1), 0)
    patch = quotient(row, held, slab)
    image = row - patch * held
    index = patch
    for k in range(held):
        index = index + jnp.where(image == k, rank_ref[k] * PAD, 0)
    o_ref[...] = matmul(one_hot(index, x_ref.shape[0]), x_ref[...]).astype(o_ref.dtype)


def unpack(dest_rank, inbound, held, slab):
    return pl.pallas_call(
        functools.partial(unpack_kernel, held, slab),
        in_specs=[SCALARS, pl.BlockSpec(memory_space=pltpu.VMEM)],
        out_shape=jax.ShapeDtypeStruct((held * slab, inbound.shape[1]), inbound.dtype),
        compiler_params=FULL,
    )(dest_rank, inbound)


def slopes_kernel(normed_ref, up_ref, o_ref):
    _, o_ref[...] = gelu_both(matmul(normed_ref[...], up_ref[...]))


def own_slopes(normed, up_weight):
    rows, width = normed.shape
    hidden = up_weight.shape[1]
    tile = min(TILE, hidden)
    return pl.pallas_call(
        slopes_kernel,
        grid=(hidden // tile,),
        in_specs=[
            pl.BlockSpec((rows, width), lambda i: (0, 0)),
            pl.BlockSpec((width, tile), lambda i: (0, i)),
        ],
        out_specs=pl.BlockSpec((rows, tile), lambda i: (0, i)),
        out_shape=jax.ShapeDtypeStruct((rows, hidden), jnp.float32),
        compiler_params=FULL,
        cost_estimate=pl.CostEstimate(
            flops=2 * rows * width * hidden,
            bytes_accessed=2 * width * (hidden + rows) + 4 * rows * hidden,
            transcendentals=rows * hidden,
        ),
    )(normed, up_weight)


def own_index(codes_ref, rows, capacity, held, slab):
    groups = codes_ref.shape[0]
    turn, patch, slot = own_places(rows, capacity, slab)
    block = held * slab
    fars = groups // 2
    rep = lax.axis_index("rep").astype(jnp.int32)
    core = jnp.bitwise_and(turn, 1)
    across = jnp.right_shift(turn, 1)
    index = jnp.full((rows, 1), -1, jnp.int32)
    base = (across * 2 + core) * (fars * block) + patch * held
    for e in range(groups):
        code = codes_ref[e, 0, 0]
        owned = jnp.where(code > 0, lax.rem(code - 1, capacity), -1)
        image = lax.div(jnp.maximum(code - 1, 0), capacity)
        away = jnp.bitwise_xor(rep, e)
        near = jnp.bitwise_and(away, 1)
        far = jnp.right_shift(away, 1)
        index = jnp.where(slot == owned, base + near * (4 * fars * block) + far * block + image, index)
    return index


def own_kernel(count, held, slab, *refs):
    codes_ref, values_ref, slopes_ref = refs[:3]
    pieces = refs[3 : 3 + count]
    up_ref, down_ref, keep_ref, away_ref, grads_ref, gain_ref = refs[3 + count : 9 + count]
    total, g_all, sems = refs[9 + count :]
    step = pl.program_id(0)

    @pl.when(step == 0)
    def _():
        for copy in copies(pieces, g_all, sems):
            copy.start()

        rows = values_ref.shape[0]
        index = own_index(codes_ref, rows, rows // (4 * slab), held, slab)
        picks = one_hot(index, g_all.shape[0])
        for copy in copies(pieces, g_all, sems):
            copy.wait()
        grads_ref[...] = matmul(picks, g_all[...]).astype(jnp.bfloat16)
        total[...] = jnp.zeros_like(total)

    grad_pre = (matmul_nt(grads_ref[...], down_ref[...]) * slopes_ref[...]).astype(jnp.bfloat16)
    total[...] += matmul_nt(grad_pre, up_ref[...])

    @pl.when(step == pl.num_programs(0) - 1)
    def _():
        centred, _ = layer_norm(values_ref[...].astype(jnp.float32))
        gain_ref[...] = jnp.sum(total[...] * centred, axis=0, keepdims=True)
        half = keep_ref.shape[0]
        keep_ref[...] = total[:half, :]
        away_ref[...] = total[half:, :].astype(jnp.bfloat16)


def own_rows(codes, values, slopes, pieces, up_weight, down_weight, held, slab):
    rows, width = values.shape
    hidden = up_weight.shape[1]
    tile = hidden // 2 if hidden % (2 * LANES) == 0 else min(TILE, hidden)
    whole = lambda x: pl.BlockSpec(x.shape, lambda i: (0, 0))
    size = pieces[0].shape[0] * len(pieces)
    return pl.pallas_call(
        functools.partial(own_kernel, len(pieces), held, slab),
        grid=(hidden // tile,),
        in_specs=[SCALARS, whole(values), pl.BlockSpec((rows, tile), lambda i: (0, i))]
        + [ANYWHERE] * len(pieces)
        + [
            pl.BlockSpec((width, tile), lambda i: (0, i)),
            pl.BlockSpec((tile, width), lambda i: (i, 0)),
        ],
        out_specs=[
            pl.BlockSpec((rows // 2, width), lambda i: (0, 0)),
            pl.BlockSpec((rows // 2, width), lambda i: (0, 0)),
            pl.BlockSpec((rows, width), lambda i: (0, 0)),
            pl.BlockSpec((1, width), lambda i: (0, 0)),
        ],
        out_shape=[
            jax.ShapeDtypeStruct((rows // 2, width), jnp.float32),
            jax.ShapeDtypeStruct((rows // 2, width), jnp.bfloat16),
            jax.ShapeDtypeStruct((rows, width), jnp.bfloat16),
            jax.ShapeDtypeStruct((1, width), jnp.float32),
        ],
        scratch_shapes=[
            pltpu.VMEM((rows, width), jnp.float32),
            pltpu.VMEM((size, width), jnp.bfloat16),
            pltpu.SemaphoreType.DMA((len(pieces),)),
        ],
        compiler_params=FULL,
        cost_estimate=pl.CostEstimate(
            flops=2 * rows * width * (2 * hidden + size),
            bytes_accessed=2 * width * (2 * hidden + size + 4 * rows),
            transcendentals=rows * hidden,
        ),
    )(codes, values, slopes, *pieces, up_weight, down_weight)


def weights_kernel(count, first, *refs):
    n_refs, g_refs = refs[:count], refs[count : 2 * count]
    up_ref, down_ref = refs[2 * count : 2 * count + 2]
    rest = refs[2 * count + 2 :]
    if not first:
        up_in, down_in = rest[:2]
        rest = rest[2:]
    up_out, down_out, n_all, g_all, wide, n_sems, g_sems = rest
    width = n_refs[0].shape[1]
    share = up_out.shape[0]
    window = wide.shape[0]

    step = pl.program_id(0)

    @pl.when(step == 0)
    def _():
        for copy in copies(n_refs, n_all, n_sems) + copies(g_refs, g_all, g_sems):
            copy.start()
        for copy in copies(n_refs, n_all, n_sems) + copies(g_refs, g_all, g_sems):
            copy.wait()

    value, slope = gelu_both(matmul(n_all[...], up_ref[...]))
    grad_pre = (matmul_nt(g_all[...], down_ref[...]) * slope).astype(jnp.bfloat16)
    start = lax.axis_index("rep").astype(jnp.int32) * share
    base = jnp.minimum(lax.div(start, LANES) * LANES, width - window)
    lanes = pl.ds(pl.multiple_of(base, LANES), window)
    picked = pl.ds(pl.multiple_of(start - base, 8), share)
    wide[...] = matmul_tn(n_all[:, lanes], grad_pre)
    up = wide[picked, :]
    if not first:
        up = up + up_in[...]
    up_out[...] = up
    wide[...] = matmul_tn(g_all[:, lanes], value.astype(jnp.bfloat16))
    down = wide[picked, :]
    if not first:
        down = down + down_in[...]
    down_out[...] = down


def weight_grads(window, n_pieces, g_pieces, up_weight, down_weight, share, before):
    size, width = n_pieces[0].shape
    count = len(n_pieces)
    rows = size * count
    hidden = up_weight.shape[1]
    tile = min(TILE, hidden)
    sum_spec = pl.BlockSpec((share, tile), lambda i: (0, i))
    pieces = list(n_pieces) + list(g_pieces)
    return pl.pallas_call(
        functools.partial(weights_kernel, count, before is None),
        grid=(hidden // tile,),
        in_specs=[ANYWHERE] * len(pieces)
        + [
            pl.BlockSpec((width, tile), lambda i: (0, i)),
            pl.BlockSpec((tile, width), lambda i: (i, 0)),
        ]
        + ([] if before is None else [sum_spec, sum_spec]),
        out_specs=[sum_spec, sum_spec],
        scratch_shapes=[
            pltpu.VMEM((rows, width), jnp.bfloat16),
            pltpu.VMEM((rows, width), jnp.bfloat16),
            pltpu.VMEM((window, tile), jnp.float32),
            pltpu.SemaphoreType.DMA((count,)),
            pltpu.SemaphoreType.DMA((count,)),
        ],
        out_shape=[jax.ShapeDtypeStruct((share, hidden), jnp.float32)] * 2,
        compiler_params=FULL,
        cost_estimate=pl.CostEstimate(
            flops=4 * rows * hidden * (width + window),
            bytes_accessed=4 * width * (hidden + rows) + 16 * share * hidden,
            transcendentals=rows * hidden,
        ),
    )(*pieces, up_weight, down_weight, *(before or ()))


def near_kernel(keep_ref, got_ref, near_ref, far_ref):
    half = near_ref.shape[0]
    got = got_ref[...].astype(jnp.float32)
    near_ref[...] = keep_ref[:half, :] + got[:half, :]
    far_ref[...] = (keep_ref[half:, :] + got[half:, :]).astype(jnp.bfloat16)


def add_near(keep, got):
    rows, width = keep.shape
    return pl.pallas_call(
        near_kernel,
        out_shape=(
            jax.ShapeDtypeStruct((rows // 2, width), jnp.float32),
            jax.ShapeDtypeStruct((rows // 2, width), jnp.bfloat16),
        ),
        compiler_params=FULL,
    )(keep, got)


def finish_kernel(near_ref, far_ref, values_ref, grads_ref, gain_ref, o_ref):
    centred, inv_std = layer_norm(values_ref[...].astype(jnp.float32))
    scaled = (near_ref[...] + far_ref[...].astype(jnp.float32)) * gain_ref[...][None, :]
    first = jnp.mean(scaled, axis=1, keepdims=True)
    second = jnp.mean(scaled * centred, axis=1, keepdims=True)
    result = grads_ref[...].astype(jnp.float32) + inv_std * (scaled - first - centred * second)
    o_ref[...] = result.astype(o_ref.dtype)


def finish(near, far, values, grads, gain):
    rows, width = near.shape
    top = pl.BlockSpec((rows, width), lambda i: (0, 0))
    return pl.pallas_call(
        finish_kernel,
        grid=(1,),
        in_specs=[top, top, top, top, pl.BlockSpec((width,), lambda i: (0,))],
        out_specs=top,
        out_shape=jax.ShapeDtypeStruct((rows, width), jnp.bfloat16),
        compiler_params=FULL,
    )(near, far, values, grads, gain)


def gather_plan(image_grads, dest_rank, dest_slot, saved_inputs, up_weight, down_weight, norm_gain):
    groups = lax.axis_size("rep")
    capacity, _, width = saved_inputs.shape
    held, slab = image_grads.shape[:2]
    share = width // groups

    sent = codes_sent(dest_rank, dest_slot, groups, capacity)
    codes = lax.all_to_all(sent, "rep", split_axis=0, concat_axis=0, tiled=True)

    values, normed = norm_rows(saved_inputs, norm_gain, slab)
    block = after(image_grads, normed).transpose(1, 0, 2).reshape(slab * held, width)
    g_far = spread_far(block)

    codes = after(codes, normed)
    packed = pack(codes, normed, slab, capacity)
    inbound = lax.all_to_all(
        packed.reshape(groups, PAD, width), "rep", split_axis=0, concat_axis=0, tiled=True
    )
    here = join(g_far)
    g_plane = spread_plane(here)
    block = unpack(dest_rank, inbound.reshape(groups * PAD, width), held, slab)

    n_far = spread_far(block)
    here = join(n_far)
    slopes = own_slopes(normed, up_weight)
    n_plane = spread_plane(here)
    n_pieces = spread_core(n_plane)
    g_pieces = spread_core(g_plane)

    keep, away, grads, gain_part = own_rows(
        codes, values, slopes, g_pieces, up_weight, down_weight, held, slab
    )

    cut = [gain_part] + [flip(gain_part, "tp", k) for k in range(1, 4)]
    gain_part = (cut[0] + cut[1]) + (cut[2] + cut[3])
    moved = flip(gain_part, "rep", 1)
    away = flip(away, "tp", 1)

    step = math.gcd(share, LANES)
    window = min(width, -(-(share + LANES - step) // LANES) * LANES)
    sums = None
    bit = 2
    for lo, hi in CALLS:
        sums = weight_grads(
            window, n_pieces[lo:hi], g_pieces[lo:hi], up_weight, down_weight, share, sums
        )
        if lo == 0:
            gain_part = gain_part + after(moved, sums[0])
            moved = flip(gain_part, "rep", bit)
            near, far = add_near(keep, after(away, sums[0]))
            far = flip(far, "tp", 2)
            if bit < groups // 2:
                gain_part = gain_part + after(moved, near)
                bit *= 2
                moved = flip(gain_part, "rep", bit)
    up_grads, down_grads = sums

    rows_out = finish(near, after(far, up_grads), values, grads, norm_gain)
    input_grads = rows_out.reshape(slab, capacity, width).transpose(1, 0, 2)
    gain_part = gain_part + after(moved, up_grads)
    while bit < groups // 2:
        bit *= 2
        gain_part = gain_part + flip(gain_part, "rep", bit)
    return (input_grads, up_grads, down_grads.T, gain_part[0])


CALLS = ((0, 2), (2, 8))


def solution(mesh):
    groups, cuts = mesh.shape["rep"], mesh.shape["tp"]
    in_specs = (
        P("rep", "tp", None),
        P("rep"),
        P("rep"),
        P("rep", None, None),
        P(None, "tp"),
        P("tp", None),
        P(),
    )
    out_specs = (P("rep", "tp", None), P("rep", "tp"), P("tp", "rep"), P())

    def split(local):
        return jax.shard_map(
            local, mesh=mesh, in_specs=in_specs, out_specs=out_specs, check_vma=False
        )

    gather = split(gather_plan)
    reduce = split(local_reduce)

    def run(*args):
        all_rows = args[0].shape[0] * args[0].shape[1]
        few = all_rows <= 2 * args[4].shape[1] // cuts
        return (gather if few and cuts == 4 and groups in (4, 8, 16) else reduce)(*args)

    return run
```
